512 devices in a mesh: freq: 16 (over y_hi, x, core), tm: 32 (over y_lo, z).
Axes of the slice: x: 4, y: 4 (y_hi: 2, y_lo: 2; y = y_hi * 2 + y_lo), z: 16, core: 2. Of those that a mesh axis runs over, the one named last changes fastest.
Arguments:
- signal: bfloat16 [8192, 4096], P('tm', 'freq'), may hold values from -48 to 48
- conv_first: bfloat16 [64, 9, 64, 64], P('freq'), may hold values from -0.25 to 0.25
- conv_second: bfloat16 [64, 9, 64, 64], P('freq'), may hold values from -0.25 to 0.25
- shuffle: int32 [64], replicated, may hold values from 0 to 63, each once
- blocks: int32 [8192], P('tm'), may hold values from 0 to 255, never falling along the last dimension, each value on 1 to 64 neighbouring positions
- query_weight: bfloat16 [16, 256, 128], P('freq'), may hold values from -0.25 to 0.25
- key_weight: bfloat16 [16, 256, 128], P('freq'), may hold values from -0.375 to 0.375
- value_weight: bfloat16 [16, 256, 128], P('freq'), may hold values from -0.375 to 0.375
- out_weight: bfloat16 [16, 128, 256], P('freq'), may hold values from -1.796875 to 1.796875
Outputs:
- encoded: bfloat16 [8192, 4096], P('tm', 'freq')
The draws below stay inside these ranges and needn't reach their ends.
All inputs are finite; a program needn't handle non-finite values.
Results may differ from the reference program's by a relative error of at most 0.019.
The reference program's roundings to bfloat16 on the way (of `first`, `shuffled`, `resid`, `weights` and `attended`) count: a program that leaves them out, or rounds other values in their place, can miss the bound.
Values may be sent and summed in bfloat16 or wider, within the bound.
No kernel may reach another device: no remote copies, remote signals or barrier semaphores. Data moves between devices by JAX's collectives and lax.ppermute only.
A program may use at most 128 MiB of HBM per device.

```python
import math
import jax
import jax.numpy as jnp
import numpy as np
from jax import lax

G = 64
KS = 9
HEADS = 16
HD = 128
BLK_MOST = 64
TOKENS = 8192
BAND = 256
NBLK = 256


def draw_signal(key, part):
    values = jnp.clip(jax.random.normal(jax.random.fold_in(key, 3), (TOKENS, G * G), jnp.float32), -6.0, 6.0)
    return values.astype(jnp.bfloat16)


def common_base(key):
    return jnp.clip(jax.random.normal(jax.random.fold_in(key, 7), (HEADS, BAND, HD), jnp.float32), -4.0, 4.0)


def draw_query_weight(key, part):
    return (common_base(key) / math.sqrt(BAND)).astype(jnp.bfloat16)


def draw_key_weight(key, part):
    noise = jnp.clip(jax.random.normal(jax.random.fold_in(key, 9), (HEADS, BAND, HD), jnp.float32), -4.0, 4.0)
    mixture = noise
    return (mixture / math.sqrt(BAND)).astype(jnp.bfloat16)


def steps_of(stream_key, shape, cuts, low, top_value):
    gain = 1.0
    for dim, shards_of in cuts:
        steps = jax.random.uniform(jax.random.fold_in(jax.random.fold_in(stream_key, 6), dim), (shards_of,), jnp.float32, low / len(cuts), top_value / len(cuts))
        gain = gain * jnp.repeat(jnp.exp(steps), shape[dim] // shards_of).reshape((-1,) + (1,) * (len(shape) - 1 - dim))
    return gain


def profile(amount, total, bound, slope):
    weights = [(1 << 20) // math.isqrt(rank ** slope) + 1 for rank in range(2, amount + 1)]
    surplus, counts = total - bound - (amount - 1), [1] * (amount - 1)
    while surplus > 0:
        movable = [i for i in range(amount - 1) if counts[i] < bound]
        mass, left = sum([weights[i] for i in movable]), surplus
        for i in movable:
            extra = min(bound - counts[i], max(1, left * weights[i] // mass), surplus)
            counts[i] = counts[i] + extra
            surplus = surplus - extra
    return np.array([bound] + counts)


def ragged_sizes(stream_key, count, total, reach, lean):
    if count == 2:
        one = jax.random.randint(stream_key, (), max(1, total - reach), min(reach, total - 1) + 1)
        return jnp.stack([one, total - one])
    tallies = jnp.asarray(profile(count, total, reach, lean), jnp.int32)
    twos = (count - 1) // 2
    giver, taker = tallies[1:1 + 2 * twos:2], tallies[2:2 + 2 * twos:2]
    slack = jnp.minimum(giver - 1, reach - taker)
    shifted = jax.random.randint(jax.random.fold_in(stream_key, 1), (twos,), 0, 1 << 20) % (slack + 1)
    tallies = tallies.at[1:1 + 2 * twos:2].set(giver - shifted).at[2:2 + 2 * twos:2].set(taker + shifted)
    return tallies[jax.random.permutation(jax.random.fold_in(stream_key, 2), count)]


def bell_draw(key, shape, width, limit, split=(), held_as=jnp.bfloat16):
    entries = jax.random.normal(key, shape, jnp.float32) * width
    if len(split) > 0:
        entries = steps_of(key, shape, split, -0.22, 0.18) * entries
    return jnp.clip(entries, min=-limit, max=limit).astype(held_as)


def setup_inputs(seed: int = 0) -> dict:
    key_of = jax.random.split(jax.random.key(seed), 10)
    signal = draw_signal(jax.random.fold_in(key_of[9], 71), 0)
    conv_first = bell_draw(key_of[1], (G, KS, G, G), (G * KS) ** -0.5, 0.25, ((0, 16),))
    conv_second = bell_draw(key_of[2], (G, KS, G, G), (G * KS) ** -0.5, 0.25, ((0, 16),))
    shuffle = jax.random.permutation(key_of[3], G).astype(jnp.int32)
    blocks = jnp.searchsorted(jnp.cumsum(ragged_sizes(key_of[4], NBLK, TOKENS, BLK_MOST, 1)), jnp.arange(TOKENS), side="right").astype(jnp.int32)
    query_weight = draw_query_weight(jax.random.fold_in(key_of[9], 71), 0)
    key_weight = draw_key_weight(jax.random.fold_in(key_of[9], 71), 0)
    value_weight = bell_draw(key_of[7], (HEADS, BAND, HD), BAND ** -0.5, 0.375, ((0, 16),))
    out_weight = bell_draw(key_of[8], (HEADS, HD, BAND), 0.3, 1.796875, ((0, 16),))
    return dict(signal=signal, conv_first=conv_first, conv_second=conv_second, shuffle=shuffle, blocks=blocks, query_weight=query_weight, key_weight=key_weight, value_weight=value_weight, out_weight=out_weight)


def conv_apply(data, weights, form):
    margin = KS - 1
    length = data.shape[0]
    padded = jnp.concatenate([jnp.zeros((margin,) + data.shape[1:], data.dtype), data], axis=0).astype(jnp.float32)
    result = jnp.zeros((length, data.shape[1], data.shape[2]), jnp.float32)
    for offset in range(KS):
        result = result + jnp.einsum(form, padded[margin - offset:margin - offset + length], weights[:, offset].astype(jnp.float32))
    return result

def head_attend(query_rows, key_rows, value_rows, blocks):
    span = math.gcd(TOKENS, 512)
    scale = 1.0 / math.sqrt(HD)

    def one_block(inputs):
        query_block, query_marks = inputs
        scores = jnp.dot(query_block, key_rows.T, preferred_element_type=jnp.float32) * scale
        seen = blocks[None, :] <= query_marks[:, None]
        masked = jnp.where(seen, scores, jnp.float32(-1e+30))
        peak = lax.optimization_barrier(jnp.max(masked, axis=1, keepdims=True))
        weights = jnp.where(seen, jnp.exp(masked - peak), jnp.float32(0.0))
        total = lax.optimization_barrier(jnp.sum(weights, axis=1, keepdims=True))
        summed = jnp.dot(weights.astype(jnp.bfloat16), value_rows, preferred_element_type=jnp.float32)
        return (summed / total).astype(jnp.bfloat16)
    parts = (query_rows.reshape(TOKENS // span, span, HD), blocks.reshape(TOKENS // span, span))
    return lax.map(one_block, parts).reshape(TOKENS, HD)

def reference(signal, conv_first, conv_second, shuffle, blocks, query_weight, key_weight, value_weight, out_weight):
    grid = signal.reshape(TOKENS, G, G)
    first = jax.nn.silu(conv_apply(grid, conv_first, 'tgi,gio->tgo')).astype(jnp.bfloat16)
    shuffled = first[:, :, shuffle]
    second = conv_apply(shuffled, conv_second, 'tgk,kgo->tko')
    resid = (signal.astype(jnp.float32) + second.reshape(TOKENS, G * G)).astype(jnp.bfloat16)
    bands = resid.reshape(TOKENS, HEADS, BAND).astype(jnp.float32)

    def project(weight):
        return jnp.einsum('thc,hcd->htd', bands, weight.astype(jnp.float32)).astype(jnp.bfloat16)
    queries = project(query_weight)
    keys = project(key_weight)
    values = project(value_weight)

    def per_head(inputs):
        return head_attend(inputs[0], inputs[1], inputs[2], blocks)
    attended = lax.map(per_head, (queries, keys, values))
    added = jnp.einsum('htd,hdc->thc', attended.astype(jnp.float32), out_weight.astype(jnp.float32))
    return (resid.astype(jnp.float32) + added.reshape(TOKENS, G * G)).astype(jnp.bfloat16)
```

```python
import functools
import math

import jax
import jax.numpy as jnp
from jax import lax
from jax.experimental import pallas as pl
from jax.experimental.pallas import tpu as pltpu
from jax.sharding import PartitionSpec as P

F32 = jnp.float32
BF16 = jnp.bfloat16
NEG = -1e30
FLOOR = -1e28
EXTRA = 16


def dot(a, b):
    return lax.dot_general(a, b, (((1,), (0,)), ((), ())), preferred_element_type=F32)


def dot_nt(a, b):
    return lax.dot_general(a, b, (((1,), (1,)), ((), ())), preferred_element_type=F32)


def dot_tn(a, b):
    return lax.dot_general(a, b, (((0,), (0,)), ((), ())), preferred_element_type=F32)


def iota(shape, dim):
    return lax.broadcasted_iota(jnp.int32, shape, dim)


def row_to_column(row):
    size = row.shape[1]
    square = (size, size)
    kept = jnp.where(iota(square, 0) == iota(square, 1), row, jnp.zeros_like(row))
    return jnp.sum(kept, axis=1, keepdims=True)


def column_to_row(column):
    size = column.shape[0]
    square = (size, size)
    kept = jnp.where(iota(square, 0) == iota(square, 1), column, jnp.zeros_like(column))
    return jnp.sum(kept, axis=0, keepdims=True)


def fill_diagonal(weights, wide):
    groups, taps, rows, columns = weights.shape
    width = groups * rows
    wide[...] = jnp.zeros_like(wide)
    for tap in range(taps):
        for group in range(groups):
            top = tap * width + group * rows
            wide[top : top + rows, group * columns : (group + 1) * columns] = weights[group, tap]


def fill_taps(source, taps, count, spread):
    width = source.shape[1]
    for tap in range(taps):
        start = taps - 1 - tap
        spread[:, tap * width : (tap + 1) * width] = source[start : start + count, :].astype(BF16)


def first_kernel(signal, before, weights, shuffle, out, source, spread, wide):
    groups, taps, size, _ = weights.shape
    count, width = signal.shape
    margin = taps - 1
    source[: 2 * margin, :] = before[...].astype(F32)
    source[2 * margin :, :] = signal[...].astype(F32)
    fill_diagonal(weights, wide)
    fill_taps(source, taps, count + margin, spread)
    total = dot(spread[...], wide[...])
    first = (total / (1.0 + jnp.exp(-total))).astype(BF16)
    mark = (width, size)
    chosen = jnp.where(
        iota(mark, 1) == iota(mark, 0) // groups, shuffle[...].astype(F32), jnp.zeros(mark, F32)
    )
    chosen = jnp.sum(chosen, axis=1, keepdims=True).astype(jnp.int32)
    square = (width, width)
    place = (iota(square, 0) % groups) * size + chosen
    selector = jnp.where(iota(square, 1) == place, 1.0, 0.0).astype(BF16)
    out[...] = dot_nt(selector, first).astype(BF16)


def second_kernel(
    shuffled,
    signal,
    weights,
    query_weight,
    key_weight,
    value_weight,
    blocks,
    resid_out,
    query_out,
    pair_out,
    source,
    spread,
    wide,
):
    groups, taps, size, _ = weights.shape
    count, width = signal.shape
    head = query_weight.shape[1]
    square = (width, width)
    row, column = iota(square, 0), iota(square, 1)
    target = ((row // groups) % groups) * size + (row // (groups * groups)) * groups + row % groups
    selector = jnp.where(column == target, 1.0, 0.0).astype(BF16)
    source[...] = dot_tn(shuffled[...], selector)
    fill_diagonal(weights, wide)
    fill_taps(source, taps, count, spread)
    second = dot(spread[...], wide[...])
    resid = (signal[...].astype(F32) + second).astype(BF16)
    resid_out[...] = resid
    queries = dot(resid, query_weight[...]).astype(BF16)
    marks = blocks[...].astype(F32)
    for member in range(query_out.shape[0]):
        query_out[member, :count, :] = queries
        query_out[member, count:, :] = jnp.concatenate(
            [
                jnp.broadcast_to(marks[:, k * head : (k + 1) * head], (EXTRA // 2, head))
                for k in range(2)
            ],
            axis=0,
        ).astype(BF16)
    pair_out[:count, :head] = dot(resid, key_weight[...]).astype(BF16)
    pair_out[:count, head:] = dot(resid, value_weight[...]).astype(BF16)
    pair_out[count:, :] = jnp.broadcast_to(marks, (EXTRA, width)).astype(BF16)


def attend_kernel(query_ref, *refs):
    pairs, out = refs[:-1], refs[-1]
    count = query_ref.shape[1] - EXTRA
    head = query_ref.shape[2]
    half = EXTRA // 2
    scale = 1.0 / math.sqrt(head)
    queries = query_ref[0, :count, :]
    marks = jnp.concatenate(
        [query_ref[0, count : count + 1, :], query_ref[0, count + half : count + half + 1, :]],
        axis=1,
    ).astype(F32)
    marks = row_to_column(marks)
    tiles = []
    peak = jnp.full((count, 1), FLOOR, F32)
    for pair in pairs:
        scores = dot_nt(queries, pair[:count, :head]) * scale
        seen = pair[count : count + 1, :].astype(F32) <= marks
        masked = jnp.where(seen, scores, NEG)
        peak = jnp.maximum(peak, jnp.max(masked, axis=1, keepdims=True))
        tiles.append(masked)
    total = jnp.zeros((count, 1), F32)
    summed = jnp.zeros((count, head), F32)
    for pair, masked in zip(pairs, tiles):
        weights = jnp.exp(masked - peak)
        total = total + jnp.sum(weights, axis=1, keepdims=True)
        summed = summed + dot(weights.astype(BF16), pair[:count, head:])
    out[0, :count, :] = summed
    peak_row, total_row = column_to_row(peak), column_to_row(total)
    out[0, count:, :] = jnp.concatenate(
        [
            peak_row[:, :head],
            peak_row[:, head:],
            total_row[:, :head],
            total_row[:, head:],
            jnp.zeros((4, head), F32),
        ],
        axis=0,
    )


def finish_kernel(parts, resid, out_weight, out):
    members = parts.shape[0]
    count = resid.shape[0]
    peaks, totals = [], []
    for member in range(members):
        rows = [parts[member, count + k : count + k + 1, :] for k in range(4)]
        peaks.append(row_to_column(jnp.concatenate(rows[:2], axis=1)))
        totals.append(row_to_column(jnp.concatenate(rows[2:], axis=1)))
    peak = functools.reduce(jnp.maximum, peaks)
    total = jnp.zeros_like(peak)
    summed = jnp.zeros((count, parts.shape[2]), F32)
    for member in range(members):
        factor = jnp.exp(peaks[member] - peak)
        total = total + factor * totals[member]
        summed = summed + factor * parts[member, :count, :]
    attended = (summed / total).astype(BF16)
    added = dot(attended, out_weight[...])
    out[...] = (resid[...].astype(F32) + added).astype(BF16)


def shape_of(shape, dtype):
    return jax.ShapeDtypeStruct(shape, dtype)


def ring_shift(rows, length, distance):
    return [
        (row * length + place, row * length + (place + distance) % length)
        for row in range(rows)
        for place in range(length)
    ]


def per_device(
    signal,
    conv_first,
    conv_second,
    shuffle,
    blocks,
    query_weight,
    key_weight,
    value_weight,
    out_weight,
):
    count, width = signal.shape
    groups, taps, size, _ = conv_first.shape
    margin = taps - 1
    padded = count + margin
    head = query_weight.shape[2]
    axis_size = lax.axis_size("tm")
    sources = lax.axis_size("freq")
    rows = 2
    length = axis_size // rows
    ring = length // 2
    members = [
        [row * length + 2 * place + parity for row in range(rows) for parity in range(2)]
        for place in range(ring)
    ]
    before = lax.ppermute(
        signal[count - 2 * margin :], "tm", [(i, i + 1) for i in range(axis_size - 1)]
    )
    permuted = pl.pallas_call(
        first_kernel,
        out_shape=shape_of((width, padded), BF16),
        scratch_shapes=[
            pltpu.VMEM((count + 2 * margin, width), F32),
            pltpu.VMEM((padded, taps * width), BF16),
            pltpu.VMEM((taps * width, width), BF16),
        ],
        name="first",
    )(signal, before, conv_first, shuffle.reshape(1, size))
    shuffled = lax.all_to_all(
        permuted.reshape(sources, width // sources, padded),
        "freq",
        split_axis=0,
        concat_axis=0,
        tiled=True,
    ).reshape(width, padded)
    resid, queries, pair = pl.pallas_call(
        second_kernel,
        out_shape=(
            shape_of((count, width), BF16),
            shape_of((2 * rows, count + EXTRA, head), BF16),
            shape_of((count + EXTRA, width), BF16),
        ),
        scratch_shapes=[
            pltpu.VMEM((padded, width), F32),
            pltpu.VMEM((count, taps * width), BF16),
            pltpu.VMEM((taps * width, width), BF16),
        ],
        name="second",
    )(
        shuffled,
        signal,
        conv_second,
        query_weight.reshape(width, head),
        key_weight.reshape(width, head),
        value_weight.reshape(width, head),
        blocks.reshape(1, count),
    )
    exchange = functools.partial(
        lax.all_to_all,
        axis_name="tm",
        split_axis=0,
        concat_axis=0,
        tiled=True,
        axis_index_groups=members,
    )
    queries = exchange(queries)
    pairs = [pair]
    ahead = behind = pair
    for step in range(ring // 2):
        ahead = lax.ppermute(ahead, "tm", ring_shift(rows, length, 2))
        pairs.append(ahead)
        if 2 * step + 2 < ring:
            behind = lax.ppermute(behind, "tm", ring_shift(rows, length, -2))
            pairs.append(behind)
    whole = pl.BlockSpec((count + EXTRA, width), lambda j: (0, 0))
    parts = pl.pallas_call(
        attend_kernel,
        grid=(2 * rows,),
        out_shape=shape_of((2 * rows, count + 8, head), F32),
        in_specs=[pl.BlockSpec((1, count + EXTRA, head), lambda j: (j, 0, 0))]
        + [whole] * len(pairs),
        out_specs=pl.BlockSpec((1, count + 8, head), lambda j: (j, 0, 0)),
        name="attend",
    )(queries, *pairs)
    parts = exchange(parts)
    return pl.pallas_call(
        finish_kernel,
        out_shape=shape_of((count, width), BF16),
        name="finish",
    )(parts, resid, out_weight.reshape(head, width))


def solution(mesh):
    in_specs = (
        P("tm", "freq"),
        P("freq", None, None, None),
        P("freq", None, None, None),
        P(),
        P("tm"),
        P("freq", None, None),
        P("freq", None, None),
        P("freq", None, None),
        P("freq", None, None),
    )
    return jax.shard_map(
        per_device, mesh=mesh, in_specs=in_specs, out_specs=P("tm", "freq"), check_vma=False
    )
```

```python
import functools
import math

import jax
import jax.numpy as jnp
from jax import lax
from jax.experimental import pallas as pl
from jax.experimental.pallas import tpu as pltpu
from jax.sharding import PartitionSpec as P


F32 = jnp.float32
BF16 = jnp.bfloat16
NEG = -1e30
FLOOR = -1e28
TINY = 1e-30
EXTRA = 8
STATS = 16
LIMIT = 24 * 1024 * 1024


def dot(a, b):
    return lax.dot_general(a, b, (((1,), (0,)), ((), ())), preferred_element_type=F32)


def dot_nt(a, b):
    return lax.dot_general(a, b, (((1,), (1,)), ((), ())), preferred_element_type=F32)


def dot_tn(a, b):
    return lax.dot_general(a, b, (((0,), (0,)), ((), ())), preferred_element_type=F32)


def iota(shape, dim):
    return lax.broadcasted_iota(jnp.int32, shape, dim)


def row_to_column(row):
    size = row.shape[1]
    square = (size, size)
    kept = jnp.where(iota(square, 0) == iota(square, 1), row, jnp.zeros_like(row))
    return jnp.sum(kept, axis=1, keepdims=True)


def column_to_row(column):
    size = column.shape[0]
    square = (size, size)
    kept = jnp.where(iota(square, 0) == iota(square, 1), column, jnp.zeros_like(column))
    return jnp.sum(kept, axis=0, keepdims=True)


def fill_diagonal(weights, wide):
    groups, taps, rows, columns = weights.shape
    width = groups * rows
    wide[...] = jnp.zeros_like(wide)
    for tap in range(taps):
        for group in range(groups):
            top = tap * width + group * rows
            wide[top : top + rows, group * columns : (group + 1) * columns] = weights[group, tap]


def fill_taps(source, taps, count, spread):
    width = source.shape[1]
    for tap in range(taps):
        start = taps - 1 - tap
        spread[:, tap * width : (tap + 1) * width] = source[start : start + count, :].astype(BF16)


def prepare_kernel(first, second, shuffle, first_wide, second_wide, send, receive):
    groups, _, size, _ = first.shape
    width = groups * size
    fill_diagonal(first, first_wide)
    fill_diagonal(second, second_wide)
    mark = (width, size)
    chosen = jnp.where(
        iota(mark, 1) == iota(mark, 0) // groups, shuffle[...].astype(F32), jnp.zeros(mark, F32)
    )
    chosen = jnp.sum(chosen, axis=1, keepdims=True).astype(jnp.int32)
    square = (width, width)
    row, column = iota(square, 0), iota(square, 1)
    place = (row % groups) * size + chosen
    send[...] = jnp.where(column == place, 1.0, 0.0).astype(BF16)
    target = ((row // groups) % groups) * size + (row // (groups * groups)) * groups + row % groups
    receive[...] = jnp.where(column == target, 1.0, 0.0).astype(BF16)


def first_kernel(taps, signal, before, wide, send, out, source, spread):
    count = signal.shape[0]
    margin = taps - 1
    source[: 2 * margin, :] = before[...].astype(F32)
    source[2 * margin :, :] = signal[...].astype(F32)
    fill_taps(source, taps, count + margin, spread)
    total = dot(spread[...], wide[...])
    first = (total / (1.0 + jnp.exp(-total))).astype(BF16)
    out[...] = dot_nt(send[...], first).astype(BF16)


def second_kernel(
    taps,
    shuffled,
    signal,
    wide,
    receive,
    query_weight,
    key_weight,
    value_weight,
    blocks,
    resid_out,
    query_out,
    pair_out,
    source,
    spread,
):
    count, width = signal.shape
    head = query_weight.shape[1]
    source[...] = dot_tn(shuffled[...], receive[...])
    fill_taps(source, taps, count, spread)
    second = dot(spread[...], wide[...])
    resid = (signal[...].astype(F32) + second).astype(BF16)
    resid_out[...] = resid
    queries = dot(resid, query_weight[...]).astype(BF16)
    marks = blocks[...].astype(F32)
    extra = jnp.concatenate(
        [
            jnp.broadcast_to(marks[:, k * head : (k + 1) * head], (EXTRA // 2, head))
            for k in range(2)
        ],
        axis=0,
    ).astype(BF16)
    for member in range(query_out.shape[0]):
        query_out[member, :count, :] = queries
        query_out[member, count:, :] = extra
    pair_out[:count, :head] = dot(resid, key_weight[...]).astype(BF16)
    pair_out[:count, head:] = dot(resid, value_weight[...]).astype(BF16)
    pair_out[count:, :] = jnp.broadcast_to(marks, (EXTRA, width)).astype(BF16)


def split_three(value):
    pieces = []
    for _ in range(3):
        piece = value.astype(BF16).astype(F32)
        pieces.append(piece)
        value = value - piece
    return pieces


def attend_kernel(held, fresh, last, *refs):
    query_ref, pairs = refs[0], refs[1 : 1 + fresh]
    old = refs[1 + fresh : 1 + fresh + held]
    outs = refs[1 + fresh + held :]
    members, count, head = query_ref.shape
    count = count - EXTRA
    half = EXTRA // 2
    scale = math.log2(math.e) / math.sqrt(head)
    shape = (count, head)
    halves = count // head
    for member in range(members):
        queries = query_ref[member, :count, :]
        if held:
            marks, before = old[0][member], old[1][member]
        else:
            marks = jnp.concatenate(
                [
                    query_ref[member, count : count + 1, :],
                    query_ref[member, count + half : count + half + 1, :],
                ],
                axis=1,
            ).astype(F32)
            marks = jnp.broadcast_to(row_to_column(marks), shape)
            before = jnp.full(shape, FLOOR, F32)
        tiles = []
        most = before
        for pair in pairs:
            scores = dot_nt(queries, pair[:count, :head])
            for part in range(halves):
                span = slice(part * head, (part + 1) * head)
                seen = pair[count : count + 1, span].astype(F32) <= marks
                masked = jnp.where(seen, scores[:, span], NEG)
                most = jnp.maximum(most, masked)
                tiles.append(masked)
        peak = jnp.broadcast_to(jnp.max(most, axis=1, keepdims=True), shape)
        summed = added = jnp.zeros(shape, F32)
        if held:
            factor = jnp.exp2((before - peak) * scale)
            summed = old[3][member] * factor
        for index, pair in enumerate(pairs):
            weights = []
            for masked in tiles[index * halves : (index + 1) * halves]:
                weights.append(jnp.exp2((masked - peak) * scale))
                added = added + weights[-1]
            weights = jnp.concatenate([w.astype(BF16) for w in weights], axis=1)
            summed = summed + dot(weights, pair[:count, head:])
        total = jnp.broadcast_to(jnp.sum(added, axis=1, keepdims=True), shape)
        if held:
            total = total + old[2][member] * factor
        if last:
            shared = summed / jnp.maximum(total, TINY)
            outs[0][member, :count, :] = shared.astype(BF16)
            rows = []
            for column in (peak, total):
                for piece in split_three(column_to_row(column[:, :1])):
                    rows += [piece[:, :head], piece[:, head:]]
            rows.append(jnp.zeros((STATS - len(rows), head), F32))
            outs[0][member, count:, :] = jnp.concatenate(rows, axis=0).astype(BF16)

            @pl.when(own_member() == member)
            def _():
                outs[1][...] = shared

        else:
            outs[0][member] = marks
            outs[1][member] = peak
            outs[2][member] = total
            outs[3][member] = summed


def own_member():
    place = lax.axis_index("tm")
    return 2 * (place // (lax.axis_size("tm") // 2)) + place % 2


def finish_kernel(parts, own, resid, out_weight, out):
    members = parts.shape[0]
    count = resid.shape[0]
    head = parts.shape[2]
    scale = math.log2(math.e) / math.sqrt(head)
    peaks, totals = [], []
    for member in range(members):
        stats = parts[member, count:, :].astype(F32)
        for index, kept in ((0, peaks), (6, totals)):
            pieces = [
                jnp.concatenate([stats[k : k + 1], stats[k + 1 : k + 2]], axis=1)
                for k in range(index, index + 6, 2)
            ]
            kept.append(pieces[0] + (pieces[1] + pieces[2]))
    peak = functools.reduce(jnp.maximum, peaks)
    shares = [jnp.exp2((peaks[k] - peak) * scale) * totals[k] for k in range(members)]
    whole = functools.reduce(jnp.add, shares)
    summed = jnp.zeros((count, head), F32)
    for member in range(members):
        share = row_to_column(shares[member] / whole)
        part = jnp.where(
            own_member() == member, own[...], parts[member, :count, :].astype(F32)
        )
        summed = summed + share * part
    added = dot(summed.astype(BF16), out_weight[...])
    out[...] = (resid[...].astype(F32) + added).astype(BF16)


def near(array):
    return pltpu.with_memory_space_constraint(array, pltpu.VMEM)


def call(kernel, outs, inputs, scratch=(), place=near):
    spec = pl.BlockSpec(memory_space=pltpu.VMEM) if place is near else pl.BlockSpec()
    return pl.pallas_call(
        kernel,
        out_shape=outs,
        in_specs=[spec] * len(inputs),
        out_specs=jax.tree.map(lambda _: pl.BlockSpec(memory_space=pltpu.VMEM), outs),
        scratch_shapes=scratch,
        compiler_params=pltpu.CompilerParams(vmem_limit_bytes=LIMIT if place is near else None),
    )(*[place(array) for array in inputs])


def ring_shift(rows, length, distance):
    return [
        (row * length + place, row * length + (place + distance) % length)
        for row in range(rows)
        for place in range(length)
    ]


def per_device(
    signal,
    conv_first,
    conv_second,
    shuffle,
    blocks,
    query_weight,
    key_weight,
    value_weight,
    out_weight,
):
    count, width = signal.shape
    _, taps, size, _ = conv_first.shape
    margin = taps - 1
    padded = count + margin
    head = query_weight.shape[2]
    axis_size = lax.axis_size("tm")
    sources = lax.axis_size("freq")
    rows = 2
    length = axis_size // rows
    ring = length // 2
    members = [
        [row * length + 2 * place + parity for row in range(rows) for parity in range(2)]
        for place in range(ring)
    ]
    before = lax.ppermute(
        signal[count - 2 * margin :], "tm", [(i, i + 1) for i in range(axis_size - 1)]
    )
    first_wide, second_wide, send, receive = call(
        prepare_kernel,
        [
            pltpu.VMEM((taps * width, width), BF16),
            pltpu.VMEM((taps * width, width), BF16),
            pltpu.VMEM((width, width), BF16),
            pltpu.VMEM((width, width), BF16),
        ],
        (conv_first, conv_second, shuffle.reshape(1, size)),
        place=lambda array: array,
    )
    (permuted,) = call(
        functools.partial(first_kernel, taps),
        [pltpu.VMEM((width, padded), BF16)],
        (signal, before, first_wide, send),
        [
            pltpu.VMEM((count + 2 * margin, width), F32),
            pltpu.VMEM((padded, taps * width), BF16),
        ],
    )
    shuffled = lax.all_to_all(
        permuted.reshape(sources, width // sources, padded),
        "freq",
        split_axis=0,
        concat_axis=0,
        tiled=True,
    ).reshape(width, padded)
    resid, queries, pair = call(
        functools.partial(second_kernel, taps),
        [
            pltpu.VMEM((count, width), BF16),
            pltpu.VMEM((2 * rows, count + EXTRA, head), BF16),
            pltpu.VMEM((count + EXTRA, width), BF16),
        ],
        (
            shuffled,
            signal,
            second_wide,
            receive,
            query_weight.reshape(width, head),
            key_weight.reshape(width, head),
            value_weight.reshape(width, head),
            blocks.reshape(1, count),
        ),
        [
            pltpu.VMEM((padded, width), F32),
            pltpu.VMEM((count, taps * width), BF16),
        ],
    )
    exchange = functools.partial(
        lax.all_to_all,
        axis_name="tm",
        split_axis=0,
        concat_axis=0,
        tiled=True,
        axis_index_groups=members,
    )
    state_shapes = [pltpu.VMEM((2 * rows, count, head), F32)] * 4
    last_shapes = [
        pltpu.VMEM((2 * rows, count + STATS, head), BF16),
        pltpu.VMEM((count, head), F32),
    ]

    def attend(state, fresh, last=False):
        return call(
            functools.partial(attend_kernel, len(state), len(fresh), last),
            last_shapes if last else state_shapes,
            (queries, *fresh, *state),
        )

    state, fresh = (), [pair]
    ahead = behind = pair
    for step in range(ring // 2):
        ahead = lax.ppermute(ahead, "tm", ring_shift(rows, length, 2))
        both = 2 * step + 2 < ring
        if both:
            behind = lax.ppermute(behind, "tm", ring_shift(rows, length, -2))
        if step == 0:
            queries = exchange(queries)
        else:
            state = attend(state, fresh)
            fresh = []
            if step + 1 < ring // 2:
                behind, *state = lax.optimization_barrier((behind, *state))
        fresh = fresh + ([ahead, behind] if both else [ahead])
    state = attend(state, fresh, last=True)
    parts = exchange(state[0])
    return pl.pallas_call(
        finish_kernel,
        out_shape=jax.ShapeDtypeStruct((count, width), BF16),
        name="finish",
    )(near(parts), near(state[1]), near(resid), near(out_weight.reshape(head, width)))


def solution(mesh):
    in_specs = (
        P("tm", "freq"),
        P("freq", None, None, None),
        P("freq", None, None, None),
        P(),
        P("tm"),
        P("freq", None, None),
        P("freq", None, None),
        P("freq", None, None),
        P("freq", None, None),
    )

    return jax.shard_map(
        per_device, mesh=mesh, in_specs=in_specs, out_specs=P("tm", "freq"), check_vma=False
    )
```

```python
import functools
import math

import jax
import jax.numpy as jnp
from jax import lax
from jax.experimental import pallas as pl
from jax.experimental.pallas import tpu as pltpu
from jax.sharding import PartitionSpec as P


F32 = jnp.float32
BF16 = jnp.bfloat16
NEG = -1e30
FLOOR = -1e28
TINY = 1e-30
EXTRA = 8
STATS = 16
LIMIT = 24 * 1024 * 1024


def dot(a, b):
    return lax.dot_general(a, b, (((1,), (0,)), ((), ())), preferred_element_type=F32)


def dot_nt(a, b):
    return lax.dot_general(a, b, (((1,), (1,)), ((), ())), preferred_element_type=F32)


def dot_tn(a, b):
    return lax.dot_general(a, b, (((0,), (0,)), ((), ())), preferred_element_type=F32)


def iota(shape, dim):
    return lax.broadcasted_iota(jnp.int32, shape, dim)


def row_to_column(row, width):
    square = (width, width)
    same = iota(square, 0) == iota(square, 1)
    parts = []
    for start in range(0, row.shape[1], width):
        kept = jnp.where(same, row[:, start : start + width], 0.0)
        parts.append(jnp.broadcast_to(jnp.sum(kept, axis=1, keepdims=True), square))
    return jnp.concatenate(parts, axis=0)


def column_to_row(column):
    width = column.shape[1]
    square = (width, width)
    same = iota(square, 0) == iota(square, 1)
    return [
        jnp.sum(
            jnp.where(same, column[start : start + width, :], 0.0), axis=0, keepdims=True
        )
        for start in range(0, column.shape[0], width)
    ]


def fill_diagonal(weights, wide):
    groups, taps, rows, columns = weights.shape
    width = groups * rows
    wide[...] = jnp.zeros_like(wide)
    for tap in range(taps):
        for group in range(groups):
            top = tap * width + group * rows
            wide[top : top + rows, group * columns : (group + 1) * columns] = weights[group, tap]


def fill_taps(source, taps, count, spread):
    width = source.shape[1]
    for tap in range(taps):
        start = taps - 1 - tap
        spread[:, tap * width : (tap + 1) * width] = source[start : start + count, :].astype(BF16)


def prepare_kernel(first, second, shuffle, first_wide, second_wide, send, receive):
    groups, _, size, _ = first.shape
    width = groups * size
    fill_diagonal(first, first_wide)
    fill_diagonal(second, second_wide)
    mark = (width, size)
    chosen = jnp.where(
        iota(mark, 1) == iota(mark, 0) // groups, shuffle[...].astype(F32), jnp.zeros(mark, F32)
    )
    chosen = jnp.sum(chosen, axis=1, keepdims=True).astype(jnp.int32)
    square = (width, width)
    row, column = iota(square, 0), iota(square, 1)
    place = (row % groups) * size + chosen
    send[...] = jnp.where(column == place, 1.0, 0.0).astype(BF16)
    target = ((row // groups) % groups) * size + (row // (groups * groups)) * groups + row % groups
    receive[...] = jnp.where(column == target, 1.0, 0.0).astype(BF16)


def first_kernel(taps, signal, before, wide, send, out, source, spread):
    count = signal.shape[0]
    margin = taps - 1
    source[: 2 * margin, :] = before[...].astype(F32)
    source[2 * margin :, :] = signal[...].astype(F32)
    fill_taps(source, taps, count + margin, spread)
    total = dot(spread[...], wide[...])
    first = (total / (1.0 + jnp.exp(-total))).astype(BF16)
    out[...] = dot_nt(send[...], first).astype(BF16)


def second_kernel(
    taps,
    shuffled,
    signal,
    wide,
    receive,
    key_weight,
    value_weight,
    blocks,
    resid_out,
    pair_out,
    plain_out,
    source,
    spread,
):
    count, width = signal.shape
    head = key_weight.shape[1]
    source[...] = dot_tn(shuffled[...], receive[...])
    fill_taps(source, taps, count, spread)
    second = dot(spread[...], wide[...])
    resid = (signal[...].astype(F32) + second).astype(BF16)
    resid_out[...] = resid
    marks = blocks[...].astype(F32)
    for start, weight in ((0, key_weight), (head, value_weight)):
        projected = dot(resid, weight[...]).astype(BF16)
        pair_out[:count, start : start + head] = projected
        plain_out[:, start : start + head] = projected
    pair_out[count:, :] = jnp.broadcast_to(marks, (EXTRA, width)).astype(BF16)


def query_kernel(resid, query_weight, blocks, query_out):
    count = resid.shape[0]
    head = query_weight.shape[1]
    queries = dot(resid[...], query_weight[...]).astype(BF16)
    marks = blocks[...].astype(F32)
    extra = jnp.concatenate(
        [
            jnp.broadcast_to(marks[:, k * head : (k + 1) * head], (EXTRA // 2, head))
            for k in range(2)
        ],
        axis=0,
    ).astype(BF16)
    for member in range(query_out.shape[0]):
        query_out[member, :count, :] = queries
        query_out[member, count:, :] = extra


def split_three(value):
    pieces = []
    for _ in range(3):
        piece = value.astype(BF16).astype(F32)
        pieces.append(piece)
        value = value - piece
    return pieces


def attend_kernel(held, shifts, last, *refs):
    fresh = len(shifts)
    query_ref, pairs = refs[0], refs[1 : 1 + fresh]
    old = refs[1 + fresh : 1 + fresh + held]
    outs = refs[1 + fresh + held :]
    mine = lax.axis_index("tm")
    length = lax.axis_size("tm") // 2
    ring = length // 2
    place = lax.rem(mine, length)
    group, parity = place // 2, lax.rem(place, 2)
    members, count, head = query_ref.shape
    count = count - EXTRA
    half = EXTRA // 2
    scale = math.log2(math.e) / math.sqrt(head)
    shape = (count, head)
    halves = count // head
    for member in range(members):
        queries = query_ref[member, :count, :]
        if held:
            marks, before = old[0][member], old[1][member]
        else:
            marks = jnp.concatenate(
                [
                    query_ref[member, count : count + 1, :],
                    query_ref[member, count + half : count + half + 1, :],
                ],
                axis=1,
            ).astype(F32)
            marks = row_to_column(marks, head)
            before = jnp.full(shape, FLOOR, F32)
        tiles = []
        most = before
        asker = (member // 2) * length + 2 * group + member % 2
        for pair, shift in zip(pairs, shifts):
            scores = dot_nt(queries, pair[:count, :head])
            if shift is not None:
                holder = (
                    (mine // length) * length + 2 * lax.rem(group - shift + ring, ring) + parity
                )
                hidden = jnp.where(holder < asker, jnp.float32(0.0), jnp.float32(NEG))
            for part in range(halves):
                span = slice(part * head, (part + 1) * head)
                if shift is None:
                    seen = pair[count : count + 1, span].astype(F32) <= marks
                    masked = jnp.where(seen, scores[:, span], NEG)
                else:
                    masked = scores[:, span] + hidden
                most = jnp.maximum(most, masked)
                tiles.append(masked)
        peak = jnp.broadcast_to(jnp.max(most, axis=1, keepdims=True), shape)
        summed = added = jnp.zeros(shape, F32)
        if held:
            factor = jnp.exp2((before - peak) * scale)
            summed = old[3][member] * factor
        for index, pair in enumerate(pairs):
            weights = []
            for masked in tiles[index * halves : (index + 1) * halves]:
                weights.append(jnp.exp2((masked - peak) * scale))
                added = added + weights[-1]
            weights = jnp.concatenate([w.astype(BF16) for w in weights], axis=1)
            summed = summed + dot(weights, pair[:count, head:])
        total = jnp.broadcast_to(jnp.sum(added, axis=1, keepdims=True), shape)
        if held:
            total = total + old[2][member] * factor
        if last:
            shared = summed / jnp.maximum(total, TINY)
            outs[0][member, :count, :] = shared.astype(BF16)
            rows = []
            for column in (peak, total):
                both = [split_three(row) for row in column_to_row(column)]
                rows += [half[k] for k in range(3) for half in both]
            rows.append(jnp.zeros((STATS - len(rows), head), F32))
            outs[0][member, count:, :] = jnp.concatenate(rows, axis=0).astype(BF16)

            @pl.when(own_member() == member)
            def _():
                outs[1][...] = shared

        else:
            outs[0][member] = marks
            outs[1][member] = peak
            outs[2][member] = total
            outs[3][member] = summed


def own_member():
    place = lax.axis_index("tm")
    return 2 * (place // (lax.axis_size("tm") // 2)) + place % 2


def finish_kernel(parts, own, resid, out_weight, out):
    members = parts.shape[0]
    count = resid.shape[0]
    head = parts.shape[2]
    scale = math.log2(math.e) / math.sqrt(head)
    peaks, totals = [], []
    for member in range(members):
        stats = parts[member, count:, :].astype(F32)
        for index, kept in ((0, peaks), (6, totals)):
            pieces = [
                jnp.concatenate([stats[k : k + 1], stats[k + 1 : k + 2]], axis=1)
                for k in range(index, index + 6, 2)
            ]
            kept.append(pieces[0] + (pieces[1] + pieces[2]))
    peak = functools.reduce(jnp.maximum, peaks)
    shares = [jnp.exp2((peaks[k] - peak) * scale) * totals[k] for k in range(members)]
    whole = functools.reduce(jnp.add, shares)
    summed = jnp.zeros((count, head), F32)
    for member in range(members):
        share = row_to_column(shares[member] / whole, head)
        part = jnp.where(
            own_member() == member, own[...], parts[member, :count, :].astype(F32)
        )
        summed = summed + share * part
    added = dot(summed.astype(BF16), out_weight[...])
    out[...] = (resid[...].astype(F32) + added).astype(BF16)


def near(array):
    return pltpu.with_memory_space_constraint(array, pltpu.VMEM)


def call(kernel, outs, inputs, scratch=(), place=near):
    spec = pl.BlockSpec(memory_space=pltpu.VMEM) if place is near else pl.BlockSpec()
    return pl.pallas_call(
        kernel,
        out_shape=outs,
        in_specs=[spec] * len(inputs),
        out_specs=jax.tree.map(lambda _: pl.BlockSpec(memory_space=pltpu.VMEM), outs),
        scratch_shapes=scratch,
        compiler_params=pltpu.CompilerParams(vmem_limit_bytes=LIMIT if place is near else None),
    )(*[place(array) for array in inputs])


def ring_shift(rows, length, distance):
    return [
        (row * length + place, row * length + (place + distance) % length)
        for row in range(rows)
        for place in range(length)
    ]


def per_device(
    signal,
    conv_first,
    conv_second,
    shuffle,
    blocks,
    query_weight,
    key_weight,
    value_weight,
    out_weight,
):
    count, width = signal.shape
    _, taps, size, _ = conv_first.shape
    margin = taps - 1
    padded = count + margin
    head = query_weight.shape[2]
    axis_size = lax.axis_size("tm")
    sources = lax.axis_size("freq")
    rows = 2
    length = axis_size // rows
    ring = length // 2
    members = [
        [row * length + 2 * place + parity for row in range(rows) for parity in range(2)]
        for place in range(ring)
    ]
    before = lax.ppermute(
        signal[count - 2 * margin :], "tm", [(i, i + 1) for i in range(axis_size - 1)]
    )
    first_wide, second_wide, send, receive = call(
        prepare_kernel,
        [
            pltpu.VMEM((taps * width, width), BF16),
            pltpu.VMEM((taps * width, width), BF16),
            pltpu.VMEM((width, width), BF16),
            pltpu.VMEM((width, width), BF16),
        ],
        (conv_first, conv_second, shuffle.reshape(1, size)),
        place=lambda array: array,
    )
    (permuted,) = call(
        functools.partial(first_kernel, taps),
        [pltpu.VMEM((width, padded), BF16)],
        (signal, before, first_wide, send),
        [
            pltpu.VMEM((count + 2 * margin, width), F32),
            pltpu.VMEM((padded, taps * width), BF16),
        ],
    )
    shuffled = lax.all_to_all(
        permuted.reshape(sources, width // sources, padded),
        "freq",
        split_axis=0,
        concat_axis=0,
        tiled=True,
    ).reshape(width, padded)
    resid, pair, plain = call(
        functools.partial(second_kernel, taps),
        [
            pltpu.VMEM((count, width), BF16),
            pltpu.VMEM((count + EXTRA, width), BF16),
            pltpu.VMEM((count, width), BF16),
        ],
        (
            shuffled,
            signal,
            second_wide,
            receive,
            key_weight.reshape(width, head),
            value_weight.reshape(width, head),
            blocks.reshape(1, count),
        ),
        [
            pltpu.VMEM((padded, width), F32),
            pltpu.VMEM((count, taps * width), BF16),
        ],
    )
    exchange = functools.partial(
        lax.all_to_all,
        axis_name="tm",
        split_axis=0,
        concat_axis=0,
        tiled=True,
        axis_index_groups=members,
    )
    state_shapes = [pltpu.VMEM((2 * rows, count, head), F32)] * 4
    last_shapes = [
        pltpu.VMEM((2 * rows, count + STATS, head), BF16),
        pltpu.VMEM((count, head), F32),
    ]

    def attend(state, fresh, step):
        last = step == ring // 2
        fresh, shifts = zip(*fresh)
        return call(
            functools.partial(attend_kernel, len(state), shifts, last),
            last_shapes if last else state_shapes,
            (queries, *fresh, *state),
        )

    state, fresh = (), [(pair, None)]
    ahead, behind = plain, pair
    for step in range(ring // 2):
        ahead = lax.ppermute(ahead, "tm", ring_shift(rows, length, 2))
        both = 2 * step + 2 < ring
        if both:
            behind = lax.ppermute(behind, "tm", ring_shift(rows, length, -2))
        if step == 0:
            (queries,) = call(
                query_kernel,
                [pltpu.VMEM((2 * rows, count + EXTRA, head), BF16)],
                (resid, query_weight.reshape(width, head), blocks.reshape(1, count)),
            )
            queries = exchange(queries)
        else:
            state = attend(state, fresh, step)
            fresh = []
            if step + 1 < ring // 2:
                behind, *state = lax.optimization_barrier((behind, *state))
        fresh = fresh + [(ahead, step + 1)] + ([(behind, None)] if both else [])
    state = attend(state, fresh, ring // 2)
    parts = exchange(state[0])
    return pl.pallas_call(
        finish_kernel,
        out_shape=jax.ShapeDtypeStruct((count, width), BF16),
        name="finish",
    )(near(parts), near(state[1]), near(resid), near(out_weight.reshape(head, width)))


def solution(mesh):
    in_specs = (
        P("tm", "freq"),
        P("freq", None, None, None),
        P("freq", None, None, None),
        P(),
        P("tm"),
        P("freq", None, None),
        P("freq", None, None),
        P("freq", None, None),
        P("freq", None, None),
    )

    return jax.shard_map(
        per_device, mesh=mesh, in_specs=in_specs, out_specs=P("tm", "freq"), check_vma=False
    )
```
